32 devices in a mesh: region: 16 (over z, y, core), tracer: 2 (over x).
Axes of the slice: x: 2, y: 2, z: 4, core: 2. Of those that a mesh axis runs over, the one named last changes fastest.
Arguments:
- tracers: float32 [256, 32, 6144], P('tracer', 'region'), may hold values from 0.2 to 1.5
- fluxes: float32 [2, 32, 6144], P(None, 'region', 'tracer'), may hold values from -0.4 to 0.4
- rate_coeff: float32 [1024], replicated, may hold values from 0.005 to 0.05
- first_reactant: int32 [1024], replicated, may hold values from 0 to 255
- second_reactant: int32 [1024], replicated, may hold values from 0 to 255
- product_species: int32 [1024], replicated, may hold values from 0 to 255
Outputs:
- tracers_out: float32 [256, 32, 6144], P('tracer', 'region')
The draws below stay inside these ranges and needn't reach their ends.
All inputs are finite; a program needn't handle non-finite values.
Results may differ from the reference program's by a relative error of at most 0.0001.
Values sent between devices are 32-bit elements; how exact they have to be, the bound alone decides.
A program may use at most 128 MiB of HBM per device.

```python
import math
import jax
import jax.numpy as jnp
from jax import lax

TRACERS = 256
REACTIONS = 1024
NY = 48
LEV = 128
CX = 2
ADV_STEPS = 2
SUBSTEPS = 4
NX = 32


def set_ends(values, rng, low, top_value):
    dims = values.shape
    place = [jax.random.randint(jax.random.fold_in(rng, axis), (), 0, dims[axis]) for axis in range(len(dims))]
    values = values.at[tuple(place)].set(low)
    longest = dims.index(max(dims))
    place[longest] = (place[longest] + 1) % dims[longest]
    return values.at[tuple(place)].set(top_value)


def steps_of(key, dims, split, least, largest):
    def one(dim, shards_of):
        steps = jax.random.uniform(jax.random.fold_in(jax.random.fold_in(key, 6), dim), (shards_of,), jnp.float32, least / len(split), largest / len(split))
        return jnp.repeat(jnp.exp(steps), dims[dim] // shards_of).reshape((-1,) + (1,) * (len(dims) - dim - 1))

    factor_of = one(*split[0])
    for cut in split[1:]:
        factor_of = factor_of * one(*cut)
    return factor_of


def setup_inputs(seed: int = 0) -> dict:
    key_list = jax.random.split(jax.random.key(seed), 7)
    tracers = jnp.clip(0.2 + 1.3 * jax.random.uniform(key_list[0], (TRACERS, NX, LEV * NY), jnp.float32) ** steps_of(key_list[0], (TRACERS, NX, LEV * NY), ((0, 2), (1, 16)), -0.2, 0.2), 0.2, 1.5)
    fluxes = jnp.clip(jax.random.uniform(key_list[1], (2, NX, LEV * NY), jnp.float32, -0.4, 0.4) * steps_of(key_list[1], (2, NX, LEV * NY), ((1, 16), (2, 2)), -0.4, 0.0), -0.4, 0.4)
    rate_coeff = jnp.clip(jnp.exp(jax.random.uniform(key_list[2], (REACTIONS,), jnp.float32, math.log(0.005), math.log(0.05))), 0.005, 0.05)
    first_reactant = set_ends(jax.random.randint(key_list[3], (REACTIONS,), 0, TRACERS), jax.random.fold_in(key_list[3], 1), 0, TRACERS - 1).astype(jnp.int32)
    second_reactant = set_ends(jax.random.randint(key_list[4], (REACTIONS,), 0, TRACERS), jax.random.fold_in(key_list[4], 1), 0, TRACERS - 1).astype(jnp.int32)
    product_species = set_ends(jax.random.randint(key_list[5], (REACTIONS,), 0, TRACERS), jax.random.fold_in(key_list[5], 1), 0, TRACERS - 1).astype(jnp.int32)
    return {"tracers": tracers, "fluxes": fluxes, "rate_coeff": rate_coeff, "first_reactant": first_reactant, "second_reactant": second_reactant, "product_species": product_species}


def advect(padded, courant, margin, wind_margin, row_len):
    length = padded.shape[1]
    offset = wind_margin - margin
    east_flow = courant[0, offset + 1: offset + length]
    flux_x = jnp.maximum(east_flow, 0.0) * padded[:, :-1] + jnp.minimum(east_flow, 0.0) * padded[:, 1:]
    central = padded[:, 1:-1]
    north_flow = courant[1, offset + 1: offset + length - 1]
    south_cell = jnp.roll(central, 1, axis=2)
    y_index = jnp.arange(central.shape[2], dtype=jnp.int32) % row_len
    flux_y = jnp.where(y_index == 0, 0.0, jnp.maximum(north_flow, 0.0) * south_cell + jnp.minimum(north_flow, 0.0) * central)
    return central + flux_x[:, :-1] - flux_x[:, 1:] + flux_y - jnp.roll(flux_y, -1, axis=2)


def tables(first_reactant, second_reactant, product_species, count):
    species = jnp.arange(count, dtype=jnp.int32)
    pick_first = (first_reactant[:, None] == species[None, :]).astype(jnp.float32)
    pick_second = (second_reactant[:, None] == species[None, :]).astype(jnp.float32)
    made = (product_species[:, None] == species[None, :]).astype(jnp.float32)
    change_table = jnp.transpose(made - pick_first - pick_second)
    return pick_first, pick_second, change_table


def chemistry_steps(amounts, rate_coeff, pick_first, pick_second, change_table):
    for repeat in range(SUBSTEPS):
        first = jnp.dot(pick_first, amounts, precision=lax.Precision.HIGHEST)
        second = jnp.dot(pick_second, amounts, precision=lax.Precision.HIGHEST)
        velocity = rate_coeff[:, None] * first * second
        amounts = amounts + jnp.dot(change_table, velocity, precision=lax.Precision.HIGHEST)
    return amounts


def reference(tracers, fluxes, rate_coeff, first_reactant, second_reactant, product_species):
    courant = jnp.concatenate([fluxes[:, -ADV_STEPS:], fluxes, fluxes[:, :ADV_STEPS]], axis=1)
    tracer_now = tracers
    for repeat in range(ADV_STEPS):
        padded = jnp.concatenate([tracer_now[:, -1:], tracer_now, tracer_now[:, :1]], axis=1)
        tracer_now = advect(padded, courant, 1, ADV_STEPS, NY)
    pick_first, pick_second, change_table = tables(first_reactant, second_reactant, product_species, TRACERS)
    block_size = CX * LEV * NY
    by_block = jnp.transpose(tracer_now.reshape(TRACERS, -1, block_size), (1, 0, 2))

    def chemistry(portion):
        return chemistry_steps(portion, rate_coeff, pick_first, pick_second, change_table)

    reacted = lax.map(chemistry, by_block)
    return jnp.transpose(reacted, (1, 0, 2)).reshape(tracer_now.shape)
```

```python
import functools

import jax
import jax.numpy as jnp
from jax import lax
from jax.experimental import pallas as pl
from jax.experimental.pallas import tpu as pltpu
from jax.sharding import PartitionSpec as P

NY = 48
SUBSTEPS = 4
LANES = 128
BLOCKS = 3
ROWS = 2 * BLOCKS
GROUP = BLOCKS * LANES


def ring(axis, by):
    length = lax.axis_size(axis)
    return [(i, (i + by) % length) for i in range(length)]


def swap_pairs(rows, even):
    return jnp.where(even, pltpu.roll(rows, 7, 0), pltpu.roll(rows, 1, 0))


def south_north(rows, lane):
    south = pltpu.roll(rows, 1, 1)
    south = jnp.where(lane == 0, pltpu.roll(south, 2, 0), south)
    north = pltpu.roll(rows, LANES - 1, 1)
    north = jnp.where(lane == LANES - 1, pltpu.roll(north, 6, 0), north)
    return south, north


def advect_rows(own, west, east, coef, even, lane):
    edge = jnp.where(even, east, west)
    outer = jnp.where(even, west, east)

    def step(center, inner, out, base):
        south, north = south_north(center, lane)
        return (
            coef[base] * center
            + coef[base + 1] * inner
            + coef[base + 2] * out
            + coef[base + 3] * south
            + coef[base + 4] * north
        )

    own_swap = swap_pairs(own, even)
    new_own = step(own, own_swap, swap_pairs(edge, even), 0)
    new_edge = step(edge, own_swap, swap_pairs(outer, even), 5)
    return step(new_own, swap_pairs(new_own, even), swap_pairs(new_edge, even), 0)


def react_kernel(parts, groups, count, *refs):
    first_ref, second_ref, rate_ref, table_ref, coef_ref = refs[:5]
    own_refs = refs[5 : 5 + parts]
    west_refs = refs[5 + parts : 5 + 2 * parts]
    east_refs = refs[5 + 2 * parts : 5 + 3 * parts]
    out_refs = refs[5 + 3 * parts : 5 + 4 * parts]
    c_ref, w_ref = refs[5 + 4 * parts :]
    reactions = first_ref.shape[0]
    species = parts * count
    quad = 4 * groups * ROWS
    row = lax.broadcasted_iota(jnp.int32, (8, LANES), 0)
    lane = lax.broadcasted_iota(jnp.int32, (8, LANES), 1)
    even = row % 2 == 0

    def rows_of(ref, base, off):
        if off + 8 <= quad:
            return ref[pl.ds(base + off, 8), :]
        return pltpu.roll(ref[pl.ds(base + quad - 8, 8), :], 6, 0)

    for part in range(parts):
        for group in range(groups):
            coef = [coef_ref[k, group] for k in range(10)]

            def advect_four(i, carry, part=part, group=group, coef=coef):
                base = pl.multiple_of(i * quad, 8)
                for j in range(4):
                    off = (j * groups + group) * ROWS
                    values = [
                        rows_of(ref[part], base, off) for ref in (own_refs, west_refs, east_refs)
                    ]
                    start = pl.multiple_of(
                        ((part * count + i * 4 + j) * groups + group) * 8, 8
                    )
                    c_ref[pl.ds(start, 8), :] = advect_rows(*values, coef, even, lane)
                return carry

            lax.fori_loop(0, count // 4, advect_four, 0)

    height = groups * 8
    unroll = 16

    def react(step, carry):
        def velocities(i, carry):
            for j in range(unroll):
                r = i * unroll + j
                first = pl.multiple_of(first_ref[r], 8)
                second = pl.multiple_of(second_ref[r], 8)
                w_ref[pl.ds(pl.multiple_of(r * height, 8), height), :] = (
                    rate_ref[r]
                    * c_ref[pl.ds(first, height), :]
                    * c_ref[pl.ds(second, height), :]
                )
            return carry

        lax.fori_loop(0, reactions // unroll, velocities, 0)

        for group in range(groups):
            for k in range(ROWS):
                at = group * 8 + k
                w = w_ref[pl.ds(at, reactions, stride=height), :]
                high = w.astype(jnp.bfloat16)
                low = (w - high.astype(jnp.float32)).astype(jnp.bfloat16)
                change = jnp.dot(
                    table_ref[...],
                    jnp.concatenate([high, low], axis=1),
                    preferred_element_type=jnp.float32,
                )
                where = pl.ds(at, species, stride=height)
                c_ref[where, :] = c_ref[where, :] + (change[:, :LANES] + change[:, LANES:])
        return carry

    lax.fori_loop(0, SUBSTEPS, react, 0)

    for part in range(parts):

        def put_four(i, carry, part=part):
            base = pl.multiple_of(i * quad, 8)
            for j in range(4):
                for group in range(groups):
                    start = pl.multiple_of(
                        ((part * count + i * 4 + j) * groups + group) * 8, 8
                    )
                    out_refs[part][pl.ds(base + (j * groups + group) * ROWS, ROWS), :] = c_ref[
                        pl.ds(start, ROWS), :
                    ]
            return carry

        lax.fori_loop(0, count // 4, put_four, 0)


def react_chunk(first, second, rate, table, coef, own, west, east, count):
    parts = len(own)
    groups = coef.shape[1]
    reactions = first.shape[0]
    species = parts * count
    smem = pl.BlockSpec(memory_space=pltpu.SMEM)
    vmem = pl.BlockSpec(memory_space=pltpu.VMEM)
    cells = species * groups * GROUP * 2
    return pl.pallas_call(
        functools.partial(react_kernel, parts, groups, count),
        out_shape=[jax.ShapeDtypeStruct(own[0].shape, jnp.float32)] * parts,
        in_specs=[smem] * 3 + [vmem] * (2 + 3 * parts),
        out_specs=[vmem] * parts,
        scratch_shapes=[
            pltpu.VMEM((species * groups * 8, LANES), jnp.float32),
            pltpu.VMEM((reactions * groups * 8, LANES), jnp.float32),
        ],
        cost_estimate=pl.CostEstimate(
            flops=cells * reactions * 2 * 2 * SUBSTEPS, bytes_accessed=cells * 4 * 4, transcendentals=0
        ),
        compiler_params=pltpu.CompilerParams(vmem_limit_bytes=40 * 1024 * 1024),
        name=f"react_{groups}",
    )(first, second, rate, table, coef, *own, *west, *east)


def coefficients(fluxes, from_west, from_east):
    u, v = fluxes[0], fluxes[1]
    uw, vw = from_west[0], from_west[1]
    ue, ve = from_east[0], from_east[1]
    y = jnp.arange(u.shape[1], dtype=jnp.int32) % NY
    bottom, top = y == 0, y == NY - 1

    def up(values):
        return jnp.maximum(values, 0.0)

    def down(values):
        return jnp.minimum(values, 0.0)

    def rows(west_face, east_face, face_in, face_out, v_here):
        above = jnp.roll(v_here, -1, axis=1)
        center = (
            1.0
            + down(west_face)
            - up(east_face)
            + jnp.where(bottom, 0.0, down(v_here))
            - jnp.where(top, 0.0, up(above))
        )
        south = jnp.where(bottom, 0.0, up(v_here))
        north = jnp.where(top, 0.0, -down(above))
        return [center, face_in, face_out, south, north]

    u0, u1, u2, u3, um = u[0], u[1], ue[0], ue[1], uw[1]
    own = rows(
        jnp.stack([u0, u1]),
        jnp.stack([u1, u2]),
        jnp.stack([-down(u1), up(u1)]),
        jnp.stack([up(u0), -down(u2)]),
        v,
    )
    edge = rows(
        jnp.stack([u2, um]),
        jnp.stack([u3, u0]),
        jnp.stack([up(u2), -down(u0)]),
        jnp.stack([-down(u3), up(um)]),
        jnp.stack([ve[0], vw[1]]),
    )
    coef = jnp.stack(own + edge)
    count = coef.shape[0]
    coef = coef.reshape(count, 2, -1, BLOCKS, LANES).transpose(0, 2, 3, 1, 4)
    coef = coef.reshape(count, -1, ROWS, LANES)
    return jnp.pad(coef, ((0, 0), (0, 0), (0, 8 - ROWS), (0, 0)))


def chunk_sizes(total):
    if total >= 8:
        return [2, total - 4, 2]
    return [1] * total


def body(tracers, fluxes, rate_coeff, first_reactant, second_reactant, product_species):
    parts = lax.axis_size("tracer")
    me = lax.axis_index("tracer")
    count, columns, length = tracers.shape
    blocks = length // LANES
    own_blocks = blocks // parts
    species = parts * count
    natural = tracers.reshape(count, columns, blocks, LANES).transpose(0, 2, 1, 3)

    from_west = lax.ppermute(fluxes, "region", ring("region", 1))
    from_east = lax.ppermute(fluxes, "region", ring("region", -1))

    chunks, at = [], 0
    for size in chunk_sizes(own_blocks // BLOCKS):
        chunks.append((at, size))
        at += size

    def piece(source, owner, start, size):
        taken = lax.dynamic_slice_in_dim(
            source, owner * own_blocks + start * BLOCKS, size * BLOCKS, axis=1
        )
        return taken.reshape(count * size * ROWS, LANES)

    owns, wests, easts = [], [], []
    for start, size in chunks:
        pieces = [piece(natural, (me + shift) % parts, start, size) for shift in range(parts)]
        if owns:
            pieces[1:], _ = lax.optimization_barrier((pieces[1:], owns[-1][1:]))
            pieces[0], _ = lax.optimization_barrier((pieces[0], (wests[0], easts[0])))
        own = pieces[:1]
        for shift in range(1, parts):
            own.append(lax.ppermute(pieces[shift], "tracer", ring("tracer", shift)))
        owns.append(own)
        wests.append([lax.ppermute(values, "region", ring("region", 1)) for values in own])
        easts.append([lax.ppermute(values, "region", ring("region", -1)) for values in own])

    coef = coefficients(fluxes, from_west, from_east)
    def place(index):
        return (me - index // count) % parts * count + index % count

    order = jnp.arange(species, dtype=jnp.int32)[:, None]
    first, second, product = (
        place(index) for index in (first_reactant, second_reactant, product_species)
    )
    table = (
        (product[None, :] == order).astype(jnp.float32)
        - (first[None, :] == order).astype(jnp.float32)
        - (second[None, :] == order).astype(jnp.float32)
    ).astype(jnp.bfloat16)

    by_shift = [[] for _ in range(parts)]
    for (start, size), own, west, east in zip(chunks, owns, wests, easts):
        reacted = react_chunk(
            first * (size * 8),
            second * (size * 8),
            rate_coeff,
            table,
            coef[:, start : start + size],
            own,
            west,
            east,
            count,
        )
        for shift in range(parts):
            values = reacted[shift]
            if shift:
                values = lax.ppermute(values, "tracer", ring("tracer", -shift))
            by_shift[shift].append(values.reshape(count, size * BLOCKS, columns, LANES))
    pieces = []
    for owner in range(parts):
        shift = (owner - me) % parts
        for at in range(len(chunks)):
            picked = by_shift[0][at]
            for other in range(1, parts):
                picked = jnp.where(shift == other, by_shift[other][at], picked)
            pieces.append(picked)
    out = jnp.concatenate(pieces, axis=1)
    return out.transpose(0, 2, 1, 3).reshape(tracers.shape)


def solution(mesh):
    in_specs = (P("tracer", "region", None), P(None, "region", "tracer"), P(), P(), P(), P())
    out_specs = P("tracer", "region", None)
    return jax.shard_map(body, mesh=mesh, in_specs=in_specs, out_specs=out_specs, check_vma=False)
```
